32 devices in a mesh: slab: 2 (over x), blk: 16 (over z, y, core).
Axes of the slice: x: 2, y: 2, z: 4, core: 2. Of those that a mesh axis runs over, the one named last changes fastest.
Arguments:
- transmit: bfloat16 [2, 1024, 2048], P('slab', 'blk'), may hold values from -0.125 to 0.125
- reflect: bfloat16 [2, 2, 1024, 2048], P('slab', None, 'blk'), may hold values from -0.07910156 to 0.07910156
- source_amp: bfloat16 [512, 2048], P('blk'), may hold values from -6 to 6
- source_cell: int32 [512], P('blk'), may hold values from 0 to 1023
- source_slab: int32 [512], P('blk'), may hold values from 0 to 1
Outputs:
- sweep_out: float32 [2, 512, 2048], P('slab', 'blk')
The draws below stay inside these ranges and needn't reach their ends.
All inputs are finite; a program needn't handle non-finite values.
Results may differ from the reference program's by a relative error of at most 0.018.
Values may be sent and summed in bfloat16 or wider, within the bound.
A program may use at most 64 MiB of HBM per device.

```python
import jax
import jax.numpy as jnp
from jax import lax

N = 1024
SLABS = 2
SOURCES = 512
WIDTH = 256


def set_ends(entries, stream_key, least, top_value):
    longest = entries.shape.index(max(entries.shape))
    spots = []
    for shift in (0, 1):
        where = [jax.random.randint(jax.random.fold_in(stream_key, axis), (), 0, length) for axis, length in enumerate(entries.shape)]
        where[longest] = (where[longest] + shift) % entries.shape[longest]
        spots.append(tuple(where))
    return entries.at[spots[0]].set(least).at[spots[1]].set(top_value)


def level_of(stream_key, extent, cuts, smallest, high):
    loudness = 1.0
    for position, blocks in cuts:
        heights = jax.random.uniform(jax.random.fold_in(jax.random.fold_in(stream_key, 6), position), (blocks,), jnp.float32, smallest / len(cuts), high / len(cuts))
        loudness = loudness * jnp.repeat(jnp.exp(heights), extent[position] // blocks).reshape((-1,) + (1,) * (len(extent) - 1 - position))
    return loudness


def bell_draw(own_key, shape, scale, limit, cuts=(), kind=jnp.bfloat16):
    values = jax.random.normal(own_key, shape, jnp.float32) * scale
    if len(cuts) > 0:
        values = level_of(own_key, shape, cuts, -0.22, 0.18) * values
    return jnp.clip(values, min=-limit, max=limit).astype(kind)


def setup_inputs(seed: int = 0) -> dict:
    key_of = jax.random.split(jax.random.key(seed), 6)
    transmit = bell_draw(key_of[0], (SLABS, N, 2 * N), (2 * N) ** -0.5, 0.125, ((0, 2), (1, 16)))
    reflect = bell_draw(key_of[1], (SLABS, 2, N, 2 * N), (0.6 / (2 * N) ** 0.5), 0.07910156, ((0, 2), (2, 16)))
    source_amp = bell_draw(key_of[2], (SOURCES, 2 * N), 1.0, 6.0, ((0, 16),))
    source_cell = set_ends(jax.random.randint(key_of[3], (SOURCES,), 0, N), jax.random.fold_in(key_of[3], 1), 0, N - 1).astype(jnp.int32)
    source_slab = set_ends(jax.random.randint(key_of[4], (SOURCES,), 0, SLABS), jax.random.fold_in(key_of[4], 1), 0, SLABS - 1).astype(jnp.int32)
    return {"transmit": transmit, "reflect": reflect, "source_amp": source_amp, "source_cell": source_cell, "source_slab": source_slab}


def pair_form(matrix):
    half_width = matrix.shape[0]
    real_part = matrix[:, :half_width]
    imag_part = matrix[:, half_width:]
    return jnp.concatenate([matrix, jnp.concatenate([-imag_part, real_part], 1)], 0)


def transposed(matrix):
    half_width = matrix.shape[0]
    return jnp.concatenate([matrix[:, :half_width].T, matrix[:, half_width:].T], 1)


def complex_product(left_rows, right_matrix):
    return jnp.dot(left_rows, pair_form(right_matrix), preferred_element_type=jnp.float32)


def reference(transmit, reflect, source_amp, source_cell, source_slab):
    cell_index = jnp.arange(N, dtype=jnp.int32)
    offset = (cell_index[None, :] - source_cell[:, None].astype(jnp.int32)) % N
    inside = offset < WIDTH
    inside = jnp.concatenate([inside, inside], 1)
    slab_maps = []
    for slab_number in range(SLABS):
        coupling = complex_product(reflect[slab_number, 0], reflect[slab_number, 1]).astype(jnp.bfloat16)
        through = transmit[slab_number]
        slab_maps.append((through.astype(jnp.float32) + complex_product(coupling, through)).astype(jnp.bfloat16))
    forward = []
    carried = jnp.zeros((SOURCES, 2 * N), jnp.bfloat16)
    for slab_number in range(SLABS):
        keep = inside & (source_slab == slab_number)[:, None]
        forcing = jnp.where(keep, source_amp, jnp.zeros_like(source_amp))
        carried = (forcing.astype(jnp.float32) + jnp.dot(carried, pair_form(slab_maps[slab_number]), preferred_element_type=jnp.float32)).astype(jnp.bfloat16)
        forward.append(carried)
    current = forward[SLABS - 1].astype(jnp.float32)
    backward = [current]
    for slab_number in range(SLABS - 2, -1, -1):
        operand = current.astype(jnp.bfloat16)
        message = jnp.dot(operand, pair_form(transposed(slab_maps[slab_number + 1])), preferred_element_type=jnp.float32).astype(jnp.bfloat16)
        message = lax.optimization_barrier(message)
        current = forward[slab_number].astype(jnp.float32) + message.astype(jnp.float32)
        backward.append(current)
    return jnp.stack(backward[::-1])
```

```python
import functools

import jax
import jax.numpy as jnp
from jax import lax
from jax.experimental import pallas as pl
from jax.experimental.pallas import tpu as pltpu
from jax.sharding import PartitionSpec as P


def shifted(block, axis, distance):
    devices = range(lax.axis_size(axis))
    route = [(i - distance, i) for i in devices if i - distance in devices]
    return lax.ppermute(block, axis, route)


def transposed(matrix):
    half_width = matrix.shape[0]
    return jnp.concatenate([matrix[:, :half_width].T, matrix[:, half_width:].T], 1)


def complex_rows(left_rows, right_matrix):
    inner_width = right_matrix.shape[0]
    outer_width = right_matrix.shape[1] // 2
    row_count = left_rows.shape[0]
    stacked = jnp.concatenate([left_rows[:, :inner_width], left_rows[:, inner_width:]], 0)
    product = jnp.dot(stacked, right_matrix, preferred_element_type=jnp.float32)
    real_out = product[:row_count, :outer_width] - product[row_count:, outer_width:]
    imag_out = product[:row_count, outer_width:] + product[row_count:, :outer_width]
    return jnp.concatenate([real_out, imag_out], 1)


def body(transmit, reflect, source_amp, source_cell, source_slab):
    trans_local = transmit[0]
    refl_local = reflect[0]
    half_width = source_amp.shape[1] // 2
    refl_second = lax.all_gather(refl_local[1], "blk", axis=0, tiled=True)
    coupling = complex_rows(refl_local[0], refl_second).astype(jnp.bfloat16)
    start_rows = trans_local.astype(jnp.float32)
    piece_rows = lax.all_gather(trans_local, "blk", axis=0, tiled=True)
    piece_count = piece_rows.shape[0]
    real_cols = lax.slice_in_dim(coupling, 0, piece_count, axis=1)
    imag_cols = lax.dynamic_slice_in_dim(coupling, half_width, piece_count, 1)
    left_rows = jnp.concatenate([real_cols, imag_cols], 1)
    joined = (start_rows + complex_rows(left_rows, piece_rows)).astype(jnp.bfloat16)
    slab_matrix = lax.all_gather(joined, "blk", axis=0, tiled=True)
    back_matrix = transposed(slab_matrix)
    cell_index = lax.iota(jnp.int32, half_width)
    offset = (cell_index[None, :] - source_cell[:, None]) % half_width
    inside = offset < half_width // 4
    here = source_slab == lax.axis_index("slab")
    keep = inside & here[:, None]
    keep = jnp.concatenate([keep, keep], 1)
    forcing = jnp.where(keep, source_amp, jnp.zeros_like(source_amp))
    chain_length = lax.axis_size("slab")
    carried = forcing
    for sweep_step in range(chain_length - 1):
        arrived = shifted(carried, "slab", 1)
        carried = (forcing.astype(jnp.float32) + complex_rows(arrived, slab_matrix)).astype(
            jnp.bfloat16
        )
    current = carried.astype(jnp.float32)
    for sweep_step in range(chain_length - 1):
        message = complex_rows(current.astype(jnp.bfloat16), back_matrix).astype(jnp.bfloat16)
        arrived = shifted(message, "slab", -1)
        current = carried.astype(jnp.float32) + arrived.astype(jnp.float32)
    return current[None]


MESH = pl.DeviceIdType.MESH
Y = 2
CORE = 2


def pair_kernel(
    outer, t_ref, r_ref, amp_ref, cell_ref, slab_ref, out_ref,
    g_ref, left_ref, coup_ref, x_ref, base_ref, f_ref, d_ref, far_ref,
    send_sem, recv_sem, far_send, far_recv, own_sem,
):
    plane = lax.axis_index("slab")
    me = lax.axis_index("blk")
    z, y, core = me // (Y * CORE), (me // CORE) % Y, me % CORE
    last = 1
    depth = t_ref.shape[1]
    width = t_ref.shape[2] // 2
    half = width // 2
    sources = amp_ref.shape[0]
    tile = half // 2

    def blk_of(zz, yy, cc):
        return (zz * Y + yy) * CORE + cc

    z_peers = [(z + step) % outer for step in range(1, outer)]
    y_peer, c_peer, x_peer = 1 - y, 1 - core, 1 - plane

    def rows(block):
        return pl.ds(pl.multiple_of(block * depth, depth), depth)

    def at(dev, pl_id=None):
        return (plane if pl_id is None else pl_id, dev)

    def pieces(h):
        lo = h * half
        out = []
        for m, src in ((0, r_ref.at[0, 1]), (1, t_ref.at[0])):
            for part in range(2):
                out.append((src.at[:, part * width + lo:part * width + lo + half],
                            g_ref.at[m, part, rows(me)]))
        for part in range(2):
            out.append((r_ref.at[0, 0, :, part * width:(part + 1) * width],
                        left_ref.at[part * depth:(part + 1) * depth]))
        return out

    def local_piece(i):
        src, dst = pieces(1)[i]
        return pltpu.make_async_copy(src, dst, own_sem.at[i])

    def cross_piece(i):
        src, dst = pieces(0)[i]
        return pltpu.make_async_remote_copy(
            src_ref=src, dst_ref=dst, send_sem=far_send.at[i], recv_sem=far_recv.at[i],
            device_id=at(me, 0), device_id_type=MESH)

    @pl.when(plane == last)
    def _():
        for i in range(6):
            local_piece(i).start()

    barrier = pltpu.get_barrier_semaphore()
    peers = [at(blk_of(p, y, core)) for p in z_peers]
    peers += [at(blk_of(z, y_peer, core)), at(blk_of(z, y, c_peer)), at(me, x_peer)]
    for peer in peers:
        pl.semaphore_signal(barrier, inc=1, device_id=peer, device_id_type=MESH)
    pl.semaphore_wait(barrier, len(peers))

    @pl.when(plane == last)
    def _():
        for i in range(6):
            cross_piece(i).start()

    def own_ready(first, count):
        @pl.when(plane == last)
        def _():
            for i in range(first, first + count):
                local_piece(i).wait()

        @pl.when(plane != last)
        def _():
            for i in range(first, first + count):
                cross_piece(i).wait_recv()

    pending = []
    used = [0, 0, 0]

    def push(m, block, dev):
        k = used[m]
        used[m] += 1
        ref = g_ref.at[m, :, rows(block)]
        copy = pltpu.make_async_remote_copy(
            src_ref=ref, dst_ref=ref, send_sem=send_sem.at[m, k],
            recv_sem=recv_sem.at[m, block], device_id=at(dev), device_id_type=MESH)
        copy.start()
        pending.append(copy)

    def landed(m, block):
        ref = g_ref.at[m, :, rows(block)]
        pltpu.make_async_remote_copy(
            src_ref=ref, dst_ref=ref, send_sem=send_sem.at[m, 0],
            recv_sem=recv_sem.at[m, block], device_id=at(blk_of(z, y, c_peer)),
            device_id_type=MESH).wait_recv()

    y_dev, c_dev = blk_of(z, y_peer, core), blk_of(z, y, c_peer)

    def spread_own(m):
        for p in z_peers:
            push(m, me, blk_of(p, y, core))
        push(m, me, y_dev)
        push(m, me, c_dev)

    def spread_z(m):
        for p in reversed(z_peers):
            block = blk_of(p, y, core)
            landed(m, block)
            push(m, block, y_dev)
            push(m, block, c_dev)

    def spread_y(m):
        for p in [z] + z_peers[::-1]:
            block = blk_of(p, y_peer, core)
            landed(m, block)
            push(m, block, c_dev)

    def finish(m):
        for p in [z] + z_peers:
            for yy in (y, y_peer):
                landed(m, blk_of(p, yy, c_peer))

    def complex_tile(lhs, m, j):
        cols = pl.ds(pl.multiple_of(j * tile, tile), tile)
        n = lhs.shape[0] // 2
        pr = jnp.dot(lhs, g_ref[m, 0, :, cols], preferred_element_type=jnp.float32)
        pi = jnp.dot(lhs, g_ref[m, 1, :, cols], preferred_element_type=jnp.float32)
        return pr[:n] - pi[n:], pi[:n] + pr[n:]

    mine = pl.multiple_of(plane * half, half)
    other = pl.multiple_of(x_peer * half, half)

    own_ready(0, 2)
    spread_own(0)
    own_ready(2, 2)
    spread_own(1)

    eye = (lax.broadcasted_iota(jnp.int32, (sources, sources), 0)
           == lax.broadcasted_iota(jnp.int32, (sources, sources), 1))
    cell = jnp.sum(jnp.where(eye, cell_ref[...], 0), axis=1, keepdims=True)
    slab = jnp.sum(jnp.where(eye, slab_ref[...], 0), axis=1, keepdims=True)
    col = lax.broadcasted_iota(jnp.int32, (sources, width), 1)
    offset = col - cell
    offset = jnp.where(offset < 0, offset + width, offset)
    inside = offset < width // 4
    for part in range(2):
        amp = amp_ref[:, part * width:(part + 1) * width].astype(jnp.float32)
        spot = slice(part * sources, (part + 1) * sources)
        x_ref[spot, :] = jnp.where(inside & (slab == 0), amp, 0.0).astype(jnp.bfloat16)
        base_ref[spot, :] = jnp.where(inside & (slab == 1), amp, 0.0)

    spread_z(0)
    spread_y(0)
    spread_z(1)
    finish(0)
    own_ready(4, 2)

    @pl.loop(0, half // tile)
    def _(j):
        re, im = complex_tile(left_ref[...], 0, j)
        cols = pl.ds(pl.multiple_of(mine + j * tile, tile), tile)
        coup_ref[0:depth, cols] = re.astype(jnp.bfloat16)
        coup_ref[depth:2 * depth, cols] = im.astype(jnp.bfloat16)

    def swap(ref, i):
        return pltpu.make_async_remote_copy(
            src_ref=ref, dst_ref=ref, send_sem=far_send.at[i], recv_sem=far_recv.at[i],
            device_id=at(me, x_peer), device_id_type=MESH)

    coup_copy = swap(coup_ref.at[:, pl.ds(mine, half)], 6)
    coup_copy.start()
    spread_y(1)
    finish(1)
    swap(coup_ref.at[:, pl.ds(other, half)], 6).wait_recv()

    @pl.loop(0, half // tile)
    def _(j):
        re, im = complex_tile(coup_ref[...], 1, j)
        cols = pl.ds(pl.multiple_of(j * tile, tile), tile)
        here = rows(me)
        g_ref[2, 0, here, cols] = (re + g_ref[1, 0, here, cols].astype(jnp.float32)).astype(jnp.bfloat16)
        g_ref[2, 1, here, cols] = (im + g_ref[1, 1, here, cols].astype(jnp.float32)).astype(jnp.bfloat16)

    spread_own(2)
    spread_z(2)
    spread_y(2)
    finish(2)

    @pl.loop(0, half // tile)
    def _(j):
        re, im = complex_tile(x_ref[...], 2, j)
        cols = pl.ds(pl.multiple_of(mine + j * tile, tile), tile)
        f_ref[0:sources, cols] = (re + base_ref[0:sources, cols]).astype(jnp.bfloat16)
        f_ref[sources:, cols] = (im + base_ref[sources:, cols]).astype(jnp.bfloat16)

    @pl.when(plane != last)
    def _():
        swap(f_ref.at[:, pl.ds(mine, half)], 7).start()

    step_rows = width // 4

    @pl.loop(0, 4)
    def _(j):
        spots = pl.ds(pl.multiple_of(j * step_rows, step_rows), step_rows)
        lhs = f_ref[:, pl.ds(mine, half)]
        dims = (((1,), (1,)), ((), ()))
        pr = lax.dot_general(lhs, g_ref[2, 0, spots, :], dims, preferred_element_type=jnp.float32)
        pi = lax.dot_general(lhs, g_ref[2, 1, spots, :], dims, preferred_element_type=jnp.float32)
        d_ref[0:sources, spots] = (pr[:sources] - pi[sources:]).astype(d_ref.dtype)
        d_ref[sources:, spots] = (pi[:sources] + pr[sources:]).astype(d_ref.dtype)

    def message(pl_id):
        return pltpu.make_async_remote_copy(
            src_ref=d_ref, dst_ref=far_ref, send_sem=far_send.at[8], recv_sem=far_recv.at[8],
            device_id=at(me, pl_id), device_id_type=MESH)

    @pl.when(plane == last)
    def _():
        message(0).start()
        swap(f_ref.at[:, pl.ds(other, half)], 7).wait_recv()
        out_ref[:, :width] = f_ref[:sources].astype(jnp.float32)
        out_ref[:, width:] = f_ref[sources:].astype(jnp.float32)
        message(0).wait_send()
        for i in range(6):
            cross_piece(i).wait_send()

    @pl.when(plane != last)
    def _():
        message(0).wait_recv()
        for part in range(2):
            spot = slice(part * sources, (part + 1) * sources)
            total = d_ref[spot].astype(jnp.float32) + far_ref[spot].astype(jnp.float32)
            out_ref[:, part * width:(part + 1) * width] = (
                x_ref[spot].astype(jnp.float32) + total.astype(jnp.bfloat16).astype(jnp.float32))
        swap(f_ref.at[:, pl.ds(mine, half)], 7).wait_send()

    coup_copy.wait_send()
    for copy in pending:
        copy.wait_send()


def pair_body(transmit, reflect, source_amp, source_cell, source_slab):
    outer = lax.axis_size("blk") // (Y * CORE)
    sources, double = source_amp.shape
    depth = transmit.shape[1]
    width = double // 2
    sends = 4 * outer - 1
    vm = pl.BlockSpec(memory_space=pltpu.VMEM)
    hbm = pl.BlockSpec(memory_space=pl.ANY)
    bf16 = jnp.bfloat16
    out = pl.pallas_call(
        functools.partial(pair_kernel, outer),
        out_shape=jax.ShapeDtypeStruct((sources, double), jnp.float32),
        in_specs=[hbm, hbm, vm, vm, vm],
        out_specs=vm,
        scratch_shapes=[
            pltpu.VMEM((3, 2, width, width // 2), bf16),
            pltpu.VMEM((2 * depth, width), bf16),
            pltpu.VMEM((2 * depth, width), bf16),
            pltpu.VMEM((2 * sources, width), bf16),
            pltpu.VMEM((2 * sources, width), jnp.float32),
            pltpu.VMEM((2 * sources, width), bf16),
            pltpu.VMEM((2 * sources, width), bf16),
            pltpu.VMEM((2 * sources, width), bf16),
            pltpu.SemaphoreType.DMA((3, sends)),
            pltpu.SemaphoreType.DMA((3, lax.axis_size("blk"))),
            pltpu.SemaphoreType.DMA((9,)),
            pltpu.SemaphoreType.DMA((9,)),
            pltpu.SemaphoreType.DMA((6,)),
        ],
        compiler_params=pltpu.CompilerParams(
            collective_id=0, has_side_effects=True, vmem_limit_bytes=40 * 2**20),
    )(transmit, reflect, source_amp, source_cell[None], source_slab[None])
    return out[None]


def solution(mesh):
    pair = mesh.shape["slab"] == 2 and mesh.shape["blk"] % (Y * CORE) == 0
    return jax.shard_map(
        pair_body if pair else body,
        mesh=mesh,
        in_specs=(
            P("slab", "blk", None),
            P("slab", None, "blk", None),
            P("blk", None),
            P("blk"),
            P("blk"),
        ),
        out_specs=P("slab", "blk", None),
        check_vma=False,
    )
```

```python
import functools

import jax
import jax.numpy as jnp
from jax import lax
from jax.experimental import pallas as pl
from jax.experimental.pallas import tpu as pltpu
from jax.sharding import PartitionSpec as P


def shifted(block, axis, distance):
    devices = range(lax.axis_size(axis))
    route = [(i - distance, i) for i in devices if i - distance in devices]
    return lax.ppermute(block, axis, route)


def transposed(matrix):
    half_width = matrix.shape[0]
    return jnp.concatenate([matrix[:, :half_width].T, matrix[:, half_width:].T], 1)


def complex_rows(left_rows, right_matrix):
    inner_width = right_matrix.shape[0]
    outer_width = right_matrix.shape[1] // 2
    row_count = left_rows.shape[0]
    stacked = jnp.concatenate([left_rows[:, :inner_width], left_rows[:, inner_width:]], 0)
    product = jnp.dot(stacked, right_matrix, preferred_element_type=jnp.float32)
    real_out = product[:row_count, :outer_width] - product[row_count:, outer_width:]
    imag_out = product[:row_count, outer_width:] + product[row_count:, :outer_width]
    return jnp.concatenate([real_out, imag_out], 1)


def body(transmit, reflect, source_amp, source_cell, source_slab):
    trans_local = transmit[0]
    refl_local = reflect[0]
    half_width = source_amp.shape[1] // 2
    refl_second = lax.all_gather(refl_local[1], "blk", axis=0, tiled=True)
    coupling = complex_rows(refl_local[0], refl_second).astype(jnp.bfloat16)
    start_rows = trans_local.astype(jnp.float32)
    piece_rows = lax.all_gather(trans_local, "blk", axis=0, tiled=True)
    piece_count = piece_rows.shape[0]
    real_cols = lax.slice_in_dim(coupling, 0, piece_count, axis=1)
    imag_cols = lax.dynamic_slice_in_dim(coupling, half_width, piece_count, 1)
    left_rows = jnp.concatenate([real_cols, imag_cols], 1)
    joined = (start_rows + complex_rows(left_rows, piece_rows)).astype(jnp.bfloat16)
    slab_matrix = lax.all_gather(joined, "blk", axis=0, tiled=True)
    back_matrix = transposed(slab_matrix)
    cell_index = lax.iota(jnp.int32, half_width)
    offset = (cell_index[None, :] - source_cell[:, None]) % half_width
    inside = offset < half_width // 4
    here = source_slab == lax.axis_index("slab")
    keep = inside & here[:, None]
    keep = jnp.concatenate([keep, keep], 1)
    forcing = jnp.where(keep, source_amp, jnp.zeros_like(source_amp))
    chain_length = lax.axis_size("slab")
    carried = forcing
    for sweep_step in range(chain_length - 1):
        arrived = shifted(carried, "slab", 1)
        carried = (forcing.astype(jnp.float32) + complex_rows(arrived, slab_matrix)).astype(
            jnp.bfloat16
        )
    current = carried.astype(jnp.float32)
    for sweep_step in range(chain_length - 1):
        message = complex_rows(current.astype(jnp.bfloat16), back_matrix).astype(jnp.bfloat16)
        arrived = shifted(message, "slab", -1)
        current = carried.astype(jnp.float32) + arrived.astype(jnp.float32)
    return current[None]


MESH = pl.DeviceIdType.MESH
Y = 2
CORE = 2
PLANES = 2


def pair_kernel(
    outer, t_hbm, r_hbm, amp_hbm, cell_hbm, slab_hbm, out_ref,
    amp_ref, cell_ref, slab_ref, g_ref, left_ref, coup_ref, x_ref, base_ref,
    f_ref, whole_ref, d_ref, far_ref,
    arg_sem, in_send, in_recv, left_send, left_recv, z_send, z_recv,
    c_send, c_recv, x_send, x_recv, f_send, f_recv, d_send, d_recv,
):
    plane = lax.axis_index("slab")
    me = lax.axis_index("blk")
    z, y, core = me // (Y * CORE), (me // CORE) % Y, me % CORE
    last = PLANES - 1
    depth = t_hbm.shape[1]
    width = t_hbm.shape[2] // 2
    part_width = width // (PLANES * Y)
    sources = amp_hbm.shape[0]
    y_peer, c_peer, x_peer = 1 - y, 1 - core, 1 - plane
    q = plane * Y + y
    f32, bf16 = jnp.float32, jnp.bfloat16

    def dev(p, zz, yy, cc):
        return (p, (zz * Y + yy) * CORE + cc)

    def cols(quarter, base=0):
        return pl.ds(pl.multiple_of(base + quarter * part_width, part_width), part_width)

    def remote(s, d, ss, rs, to):
        return pltpu.make_async_remote_copy(
            src_ref=s, dst_ref=d, send_sem=ss, recv_sem=rs, device_id=to, device_id_type=MESH)

    def piece(m, part, p, yy):
        s = r_hbm.at[0, 1] if m == 0 else t_hbm.at[0]
        return s.at[:, cols(p * Y + yy, part * width)]

    def slot(m, part, yy):
        return g_ref.at[m, part].at[z * Y + yy, core]

    def piece_local(m, part):
        return pltpu.make_async_copy(piece(m, part, last, y), slot(m, part, y), in_recv.at[(m * 2 + part) * Y + y])

    targets = ((0, y), (0, y_peer), (last, y_peer))

    def piece_send(m, part, k):
        p, yy = targets[k]
        return remote(piece(m, part, p, yy), slot(m, part, y), in_send.at[m, part, k],
                      in_recv.at[(m * 2 + part) * Y + y], dev(p, z, yy, core))

    def piece_recv(m, part, yy):
        return remote(slot(m, part, yy), slot(m, part, yy), in_send.at[m, part, 0],
                      in_recv.at[(m * 2 + part) * Y + yy], dev(plane, z, y_peer, core))

    def left_src(part):
        return r_hbm.at[0, 0, :, part * width:(part + 1) * width]

    def left_local(part):
        return pltpu.make_async_copy(left_src(part), left_ref.at[part].at[y], left_recv.at[part * Y + y])

    def left_push(part, k):
        to = dev(0, z, y, core) if k == 0 else dev(last, z, y_peer, core)
        return remote(left_src(part), left_ref.at[part].at[y], left_send.at[part, k],
                      left_recv.at[part * Y + y], to)

    def left_relay(part, yy):
        ref = left_ref.at[part].at[yy]
        return remote(ref, ref, left_send.at[part, 0], left_recv.at[part * Y + yy],
                      dev(plane, z, y_peer, core))

    args = [pltpu.make_async_copy(a, b, arg_sem.at[i]) for i, (a, b) in enumerate(
        ((amp_hbm, amp_ref), (cell_hbm, cell_ref), (slab_hbm, slab_ref)))]
    for copy in args:
        copy.start()

    @pl.when(plane == last)
    def _():
        for m in range(2):
            for part in range(2):
                piece_local(m, part).start()
        for part in range(2):
            left_local(part).start()

    barrier = pltpu.get_barrier_semaphore()
    peers = [dev(plane, (z + step) % outer, y, core) for step in range(1, outer)]
    peers += [dev(plane, z, y, c_peer), dev(plane, z, y_peer, core),
              dev(x_peer, z, y, core), dev(x_peer, z, y_peer, core)]
    for peer in peers:
        pl.semaphore_signal(barrier, inc=1, device_id=peer, device_id_type=MESH)
    pl.semaphore_wait(barrier, len(peers))

    @pl.when(plane == last)
    def _():
        for part in range(2):
            for k in range(3):
                piece_send(0, part, k).start()
        for part in range(2):
            for k in range(2):
                left_push(part, k).start()
        for part in range(2):
            for k in range(3):
                piece_send(1, part, k).start()

    def pieces_ready(m):
        for part in range(2):
            @pl.when(plane == last)
            def _():
                piece_local(m, part).wait()

            @pl.when(plane != last)
            def _():
                piece_recv(m, part, y).wait_recv()

            piece_recv(m, part, y_peer).wait_recv()

    pending = []
    always = plane >= 0
    steps = [s for d in range(1, outer) for s in (d, -d)]
    near = [s for s in steps if abs(s) <= 2]

    def chunk(m, zz, cc):
        return g_ref.at[m].at[:, pl.ds(zz * Y, Y), cc]

    def push(m, k, shift, to, ok):
        zz = z + shift
        ref = chunk(m, zz, core)
        copy = remote(ref, ref, z_send.at[m, k], z_recv.at[(m * outer + zz) * CORE + core], to)
        copy.start()
        pending.append((ok, m, k, shift))

    def landed(m, zz, cc):
        ref = chunk(m, zz, cc)
        remote(ref, ref, z_send.at[m, 0], z_recv.at[(m * outer + zz) * CORE + cc],
               dev(plane, z, y, c_peer)).wait_recv()

    def valid(zz):
        return (zz >= 0) & (zz < outer)

    def spread_own(m):
        for k, s in enumerate(sorted(near, key=lambda v: -abs(v))):
            ok = valid(z + s)

            @pl.when(ok)
            def _():
                push(m, k, 0, dev(plane, z + s, y, core), ok)
        push(m, 4, 0, dev(plane, z, y, c_peer), always)

    def spread(m, chosen):
        for s in chosen:
            i = steps.index(s)
            ok = valid(z + s)

            @pl.when(ok)
            def _():
                landed(m, z + s, core)
            if abs(s) >= 2:
                onward = 1 if s < 0 else -1
                both = ok & valid(z + onward)

                @pl.when(both)
                def _():
                    push(m, 5 + len(steps) + i, s, dev(plane, z + onward, y, core), both)

            @pl.when(ok)
            def _():
                push(m, 5 + i, s, dev(plane, z, y, c_peer), ok)

    def finish(m):
        for zz in range(outer):
            landed(m, zz, c_peer)

    def side(m, part):
        return g_ref[m, part].reshape(width, part_width)

    def complex_rows_here(lhs, m):
        n = lhs.shape[0] // 2
        pr = jnp.dot(lhs, side(m, 0), preferred_element_type=f32)
        pi = jnp.dot(lhs, side(m, 1), preferred_element_type=f32)
        return pr[:n] - pi[n:], pi[:n] + pr[n:]

    seconds = [s for s in steps if abs(s) == 2]
    firsts = [s for s in steps if abs(s) == 1]
    rest = [s for s in steps if abs(s) > 2]

    for copy in args:
        copy.wait()
    eye = (lax.broadcasted_iota(jnp.int32, (sources, sources), 0)
           == lax.broadcasted_iota(jnp.int32, (sources, sources), 1))
    cell = jnp.sum(jnp.where(eye, cell_ref[...], 0), axis=1, keepdims=True)
    slab = jnp.sum(jnp.where(eye, slab_ref[...], 0), axis=1, keepdims=True)
    offset = lax.broadcasted_iota(jnp.int32, (sources, width), 1) - cell
    offset = jnp.where(offset < 0, offset + width, offset)
    inside = offset < width // 4
    for part in range(2):
        amp = amp_ref[:, part * width:(part + 1) * width].astype(f32)
        x_ref[part, y] = jnp.where(inside & (slab == 0), amp, 0.0).astype(bf16)
        base_ref[part, y] = jnp.where(inside & (slab == 1), amp, 0.0).astype(bf16)

    pieces_ready(0)
    spread_own(0)

    def x_swap(yy):
        ref = x_ref.at[:, yy]
        return remote(ref, ref, x_send.at[0], x_recv.at[0], dev(plane, z, y_peer, core))

    def base_swap(yy, quarter):
        ref = base_ref.at[:, yy, :, cols(quarter)]
        return remote(ref, ref, x_send.at[1], x_recv.at[1], dev(plane, z, y_peer, core))

    x_swap(y).start()
    base_swap(y, plane * Y + y_peer).start()

    for part in range(2):
        @pl.when(plane == last)
        def _():
            left_local(part).wait()

        @pl.when(plane != last)
        def _():
            left_relay(part, y).wait_recv()
            left_relay(part, y).start()

    spread(0, seconds)
    pieces_ready(1)
    spread_own(1)
    spread(0, firsts + rest)
    finish(0)
    for part in range(2):
        left_relay(part, y_peer).wait_recv()

    re, im = complex_rows_here(left_ref[...].reshape(2 * Y * depth, width), 0)
    coup_ref[0:Y * depth, cols(q)] = re.astype(bf16)
    coup_ref[Y * depth:, cols(q)] = im.astype(bf16)
    others = ((x_peer, y), (plane, y_peer), (x_peer, y_peer))

    def coup_copy(k, quarter):
        p, yy = others[k]
        ref = coup_ref.at[:, cols(quarter)]
        return remote(ref, ref, c_send.at[k], c_recv.at[quarter], dev(p, z, yy, core))

    for k in range(3):
        coup_copy(k, q).start()
    spread(1, seconds + firsts + rest)
    finish(1)
    for k, (p, yy) in enumerate(others):
        coup_copy(k, p * Y + yy).wait_recv()

    re, im = complex_rows_here(coup_ref[...], 1)
    for part, value in ((0, re), (1, im)):
        start = g_ref[1, part, pl.ds(z * Y, Y), core].reshape(Y * depth, part_width)
        joined = (value + start.astype(f32)).astype(bf16)
        g_ref[2, part, pl.ds(z * Y, Y), core] = joined.reshape(Y, depth, part_width)
    spread_own(2)
    spread(2, seconds + firsts + rest)
    x_swap(y_peer).wait_recv()
    base_swap(y_peer, q).wait_recv()
    finish(2)

    re, im = complex_rows_here(x_ref[...].reshape(2 * Y * sources, width), 2)
    for part, value in ((0, re), (1, im)):
        start = base_ref[part, :, :, cols(q)].astype(f32)
        f_ref[part] = (value.reshape(Y, sources, part_width) + start).astype(bf16)

    lhs = f_ref[...].reshape(2 * Y * sources, part_width)
    n = Y * sources
    tile = Y * CORE * depth

    @pl.loop(0, outer)
    def _(j):
        spots = pl.ds(pl.multiple_of(j * tile, tile), tile)
        dims = (((1,), (1,)), ((), ()))
        right = [g_ref[2, part, pl.ds(j * Y, Y)].reshape(tile, part_width) for part in range(2)]
        pr = lax.dot_general(lhs, right[0], dims, preferred_element_type=f32)
        pi = lax.dot_general(lhs, right[1], dims, preferred_element_type=f32)
        d_ref[0, :, :, spots] = (pr[:n] - pi[n:]).astype(bf16).reshape(Y, sources, tile)
        d_ref[1, :, :, spots] = (pi[:n] + pr[n:]).astype(bf16).reshape(Y, sources, tile)

    def d_copy(k, yy, quarter):
        return remote(d_ref.at[:, yy], far_ref.at[quarter], d_send.at[k], d_recv.at[quarter],
                      dev(0, z, yy, core))

    def f_copy(k, yy, quarter):
        return remote(f_ref.at[:, yy], whole_ref.at[:, :, cols(quarter)], f_send.at[k],
                      f_recv.at[quarter], dev(last, z, yy, core))

    d_copy(0, y_peer, q).start()

    @pl.when(plane == last)
    def _():
        d_copy(1, y, q).start()

    f_copy(0, y_peer, q).start()

    @pl.when(plane != last)
    def _():
        f_copy(1, y, q).start()

    @pl.when(plane == last)
    def _():
        whole_ref[:, :, cols(q)] = f_ref[:, y]
        for p, yy in others:
            f_copy(0, y, p * Y + yy).wait_recv()
        for part in range(2):
            out_ref[:, part * width:(part + 1) * width] = whole_ref[part].astype(f32)

    @pl.when(plane != last)
    def _():
        for p, yy in others:
            d_copy(0, y, p * Y + yy).wait_recv()
        for part in range(2):
            total = d_ref.at[part][y].astype(f32)
            for p, yy in others:
                total = total + far_ref.at[p * Y + yy][part].astype(f32)
            out_ref[:, part * width:(part + 1) * width] = (
                x_ref.at[part][y].astype(f32) + total.astype(bf16).astype(f32))

    @pl.when(plane == last)
    def _():
        d_copy(1, y, q).wait_send()
        for m in range(2):
            for part in range(2):
                for k in range(3):
                    piece_send(m, part, k).wait_send()
        for part in range(2):
            for k in range(2):
                left_push(part, k).wait_send()

    @pl.when(plane != last)
    def _():
        f_copy(1, y, q).wait_send()
        for part in range(2):
            left_relay(part, y).wait_send()

    d_copy(0, y_peer, q).wait_send()
    f_copy(0, y_peer, q).wait_send()
    x_swap(y).wait_send()
    base_swap(y, plane * Y + y_peer).wait_send()
    for k in range(3):
        coup_copy(k, q).wait_send()
    for ok, m, k, shift in pending:
        @pl.when(ok)
        def _():
            ref = chunk(m, z + shift, core)
            remote(ref, ref, z_send.at[m, k], z_recv.at[(m * outer + z + shift) * CORE + core],
                   dev(plane, z, y, c_peer)).wait_send()


def pair_body(transmit, reflect, source_amp, source_cell, source_slab):
    outer = lax.axis_size("blk") // (Y * CORE)
    sources, double = source_amp.shape
    depth = transmit.shape[1]
    width = double // 2
    quarter = width // (PLANES * Y)
    bf16 = jnp.bfloat16
    hbm = pl.BlockSpec(memory_space=pltpu.HBM)
    sem = pltpu.SemaphoreType.DMA
    out = pl.pallas_call(
        functools.partial(pair_kernel, outer),
        out_shape=jax.ShapeDtypeStruct((sources, double), jnp.float32),
        in_specs=[hbm] * 5,
        out_specs=pl.BlockSpec(memory_space=pltpu.VMEM),
        scratch_shapes=[
            pltpu.VMEM((sources, double), bf16),
            pltpu.VMEM((1, sources), jnp.int32),
            pltpu.VMEM((1, sources), jnp.int32),
            pltpu.VMEM((3, 2, outer * Y, CORE, depth, quarter), bf16),
            pltpu.VMEM((2, Y, depth, width), bf16),
            pltpu.VMEM((2 * Y * depth, width), bf16),
            pltpu.VMEM((2, Y, sources, width), bf16),
            pltpu.VMEM((2, Y, sources, width), bf16),
            pltpu.VMEM((2, Y, sources, quarter), bf16),
            pltpu.VMEM((2, sources, width), bf16),
            pltpu.VMEM((2, Y, sources, width), bf16),
            pltpu.VMEM((PLANES * Y, 2, sources, width), bf16),
            sem((3,)),
            sem((2, 2, 3)),
            sem((2 * 2 * Y,)),
            sem((2, 2)),
            sem((2 * Y,)),
            sem((3, 5 + 4 * (outer - 1))),
            sem((3 * outer * CORE,)),
            sem((3,)),
            sem((PLANES * Y,)),
            sem((2,)),
            sem((2,)),
            sem((2,)),
            sem((PLANES * Y,)),
            sem((2,)),
            sem((PLANES * Y,)),
        ],
        compiler_params=pltpu.CompilerParams(
            collective_id=0, has_side_effects=True, vmem_limit_bytes=67043328),
    )(transmit, reflect, source_amp, source_cell[None], source_slab[None])
    return out[None]


def solution(mesh):
    pair = mesh.shape["slab"] == PLANES and mesh.shape["blk"] % (Y * CORE) == 0
    return jax.shard_map(
        pair_body if pair else body,
        mesh=mesh,
        in_specs=(
            P("slab", "blk", None),
            P("slab", None, "blk", None),
            P("blk", None),
            P("blk"),
            P("blk"),
        ),
        out_specs=P("slab", "blk", None),
        check_vma=False,
    )
```
